256 devices in a mesh: op: 16 (over x_lo, y, core), sec: 16 (over x_hi, z).
Axes of the slice: x: 4 (x_hi: 2, x_lo: 2; x = x_hi * 2 + x_lo), y: 4, z: 8, core: 2. Of those that a mesh axis runs over, the one named last changes fastest.
Arguments:
- psi: bfloat16 [16, 512, 512], P('sec'), may hold values from -6 to 6
- left_env: bfloat16 [128, 16, 512, 512], P('op', 'sec'), may hold values from -0.375 to 0.375
- right_env: bfloat16 [128, 16, 512, 512], P('op', 'sec'), may hold values from -0.25 to 0.25
- pair_code: int32 [128], P('op'), may hold values from 0 to 2
- sketch: bfloat16 [16, 512, 128], P('sec'), may hold values from -0.25 to 0.25
Outputs:
- sigma: bfloat16 [512, 8192], P('op', 'sec')
- basis: float32 [512, 2048], P('op', 'sec')
The draws below stay inside these ranges and needn't reach their ends.
All inputs are finite; a program needn't handle non-finite values.
Results may differ from the reference program's by a relative error of at most 0.0055.
Values may be sent and summed in bfloat16 or wider, within the bound.
No kernel may reach another device: no remote copies, remote signals or barrier semaphores. Data moves between devices by JAX's collectives and lax.ppermute only.
A program may use at most 64 MiB of HBM per device.

```python
import math
import jax
import jax.numpy as jnp
from jax import lax

BLK = 512
KS = 128
TERMS = 128
NSEC = 16


def touch_ends(array, stream_key, smallest, largest):
    dims = array.shape
    index_at = [jax.random.randint(jax.random.fold_in(stream_key, axis), (), 0, dims[axis]) for axis in range(len(dims))]
    array = array.at[tuple(index_at)].set(smallest)
    longest = dims.index(max(dims))
    index_at[longest] = (index_at[longest] + 1) % dims[longest]
    return array.at[tuple(index_at)].set(largest)


def with_spikes(entries, own_key, source, target, parts, factor):
    owner, partner = [(jnp.arange(entries.shape[axis_at]) // (entries.shape[axis_at] // parts)).reshape([-1 if axis == axis_at else 1 for axis in range(entries.ndim)]) for axis_at in (source, target)]
    chosen = jax.random.permutation(own_key, parts)[partner]
    strong = (owner == chosen) | (owner == (partner + parts // 2) % parts)
    return jnp.where(strong, factor * entries, entries)


def block_scale(rng, extent, shards, smallest, top_value):
    def one(position, blocks):
        steps = jax.random.uniform(jax.random.fold_in(jax.random.fold_in(rng, 6), position), (blocks,), jnp.float32, smallest / len(shards), top_value / len(shards))
        return jnp.repeat(jnp.exp(steps), extent[position] // blocks).reshape((-1,) + (1,) * (len(extent) - position - 1))

    level = one(*shards[0])
    for cut in shards[1:]:
        level = level * one(*cut)
    return level


def gaussian(own_key, dims, width, limit, pieces=(), kind=jnp.bfloat16):
    values = jax.random.normal(own_key, dims, jnp.float32) * width
    if len(pieces) > 0:
        values = block_scale(own_key, dims, pieces, -0.22, 0.18) * values
    return jnp.clip(values, min=-limit, max=limit).astype(kind)


def gaussian_with(key, dims, spread, most, pieces, heavy, held_as=jnp.bfloat16):
    result = spread * jax.random.normal(key, dims, jnp.float32)
    if pieces:
        result = result * block_scale(key, dims, pieces, -0.22, 0.18)
    return jnp.clip(with_spikes(result, jax.random.fold_in(key, 3), *heavy), -most, most).astype(held_as)


def setup_inputs(seed: int = 0) -> dict:
    key_of = jax.random.split(jax.random.key(seed), 6)
    psi = gaussian(key_of[0], (NSEC, BLK, BLK), 1.0, 6.0, ((0, 16),))
    left_env = gaussian_with(key_of[1], (TERMS, NSEC, BLK, BLK), BLK ** -0.5, 0.375, ((0, 16), (1, 16)), (0, 2, 16, 2.0))
    right_env = gaussian(key_of[2], (TERMS, NSEC, BLK, BLK), BLK ** -0.5, 0.25, ((0, 16), (1, 16)))
    pair_code = touch_ends(jax.random.randint(key_of[3], (TERMS,), 0, 3), jax.random.fold_in(key_of[3], 1), 0, 2).astype(jnp.int32)
    sketch = gaussian(key_of[4], (NSEC, BLK, KS), BLK ** -0.5, 0.25, ((0, 16),))
    return dict(psi=psi, left_env=left_env, right_env=right_env, pair_code=pair_code, sketch=sketch)


def reference(psi, left_env, right_env, pair_code, sketch):
    padded = jnp.pad(psi, ((1, 1), (0, 0), (0, 0)))

    def one_term(total, items):
        left, right, code = items
        source = lax.dynamic_slice_in_dim(padded, (2 - code).astype(jnp.int32), NSEC, 0)
        inner = jnp.einsum('cab,cbd->cad', left.astype(jnp.float32), source.astype(jnp.float32)).astype(jnp.bfloat16)
        total = total + jnp.einsum('cad,cde->cae', inner.astype(jnp.float32), right.astype(jnp.float32))
        return (total, None)
    start_sum = jnp.zeros((NSEC, BLK, BLK), jnp.float32)
    total, unused = lax.scan(one_term, start_sum, (left_env, right_env, pair_code))
    block = (total / math.sqrt(TERMS)).astype(jnp.bfloat16)
    sigma = block.transpose(1, 0, 2).reshape(BLK, NSEC * BLK)
    sampled = jnp.einsum('cad,cdk->cak', block.astype(jnp.float32), sketch.astype(jnp.float32), precision=lax.Precision.HIGHEST)
    gram = jnp.einsum('cak,cal->ckl', sampled, sampled, precision=lax.Precision.HIGHEST)
    lower = jnp.linalg.cholesky(gram)
    solved = lax.linalg.triangular_solve(lower, sampled, left_side=False, lower=True, transpose_a=True)
    basis = math.sqrt(BLK) * solved.transpose(1, 0, 2).reshape(BLK, NSEC * KS)
    return (sigma, basis)
```

```python
import functools
import math

import jax
import jax.numpy as jnp
from jax import lax
from jax.experimental import pallas as pl
from jax.experimental.pallas import tpu as pltpu
from jax.sharding import PartitionSpec as P

BF = jnp.bfloat16
F32 = jnp.float32


def main_kernel(code, core, psi, near, far, left, right, sketch, mine, other, acc, inner):
    t = pl.program_id(0)
    k = code[t]
    first = jnp.where(core[0] == 0, 2, 0)

    def times(source):
        inner[...] = jnp.dot(left[0, 0], source[...], preferred_element_type=F32).astype(BF)

    pl.when(k == 1)(lambda: times(psi))
    pl.when(k == first)(lambda: times(near))
    pl.when(k == 2 - first)(lambda: times(far))
    part = jnp.dot(inner[...], right[0, 0], preferred_element_type=F32)

    @pl.when(t == 0)
    def _():
        acc[...] = part

    @pl.when(t > 0)
    def _():
        acc[...] += part

    @pl.when(t == pl.num_programs(0) - 1)
    def _():
        c = core[0]
        scale = 1.0 / math.sqrt(128)
        for p in range(8):
            for half, ref in ((c, mine), (1 - c, other)):
                start = pl.multiple_of((2 * p + half) * 32, 32)
                rows = acc[pl.ds(start, 32), :] * scale
                some = jnp.dot(rows.astype(BF), sketch[...], preferred_element_type=F32)
                ref[pl.ds(32 * p, 32), :512] = rows.astype(ref.dtype)
                ref[pl.ds(32 * p, 32), 512:] = some.astype(ref.dtype)


def pack_kernel(mine, got, out):
    for p in range(8):
        rows = pl.ds(32 * p, 32)
        for j in range(4):
            cols = pl.ds(128 * j, 128)
            out[p, 32 * j : 32 * j + 32, :] = (mine[rows, cols] + got[rows, cols].astype(F32)).astype(BF)
    some = (mine[:, 512:] + got[:, 512:].astype(F32)).astype(BF)
    for p in range(8):
        out[p, 128:, :] = some


def sum_kernel(place, got, sigma, half, gram):
    for j in range(4):
        rows = pl.ds(32 * j, 32)
        total = got[0, rows, :].astype(F32)
        for p in range(1, 8):
            total += got[p, rows, :].astype(F32)
        sigma[:, 128 * j : 128 * j + 128] = total.astype(BF)
    total = got[0, 128:, :].astype(F32)
    for p in range(1, 8):
        total += got[p, 128:, :].astype(F32)
    gram[...] = lax.dot_general(
        total, total, (((0,), (0,)), ((), ())), precision=lax.Precision.HIGHEST, preferred_element_type=F32
    )
    half[...] = total


def exchanged(n_op, n_sec):
    pairs = []
    for s in range(n_sec - 1):
        flip = 8 if s == n_sec // 2 - 1 else 0
        for o in range(n_op):
            low, high = (o ^ flip) * n_sec + s, o * n_sec + s + 1
            if o % 2 == 0:
                pairs.append((low, high))
            else:
                pairs.append(((o ^ flip) * n_sec + s + 1, o * n_sec + s))
    return pairs


def body(psi, left_env, right_env, pair_code, sketch):
    terms = left_env.shape[0]
    n_op, n_sec = lax.axis_size("op"), lax.axis_size("sec")
    swap = [(i, i ^ 1) for i in range(n_op)]
    place = lax.axis_index("op")
    core = (place % 2).astype(jnp.int32).reshape(1)
    near = lax.ppermute(psi[0], ("op", "sec"), exchanged(n_op, n_sec))
    far = lax.ppermute(near, "op", swap)
    smem = pl.BlockSpec(memory_space=pltpu.SMEM)
    vmem = pl.BlockSpec(memory_space=pltpu.VMEM)
    big = pl.BlockSpec((1, 1, 512, 512), lambda t: (t, 0, 0, 0))
    mine, other = pl.pallas_call(
        main_kernel,
        grid=(terms,),
        in_specs=[smem, smem, vmem, vmem, vmem, big, big, vmem],
        out_specs=[vmem, vmem],
        out_shape=[jax.ShapeDtypeStruct((256, 640), F32), jax.ShapeDtypeStruct((256, 640), BF)],
        scratch_shapes=[pltpu.VMEM((512, 512), F32), pltpu.VMEM((512, 512), BF)],
        compiler_params=pltpu.CompilerParams(vmem_limit_bytes=24 * 2**20),
        name="main",
    )(pair_code, core, psi[0], near, far, left_env, right_env, sketch[0])
    got = lax.ppermute(other, "op", swap)
    packed = pl.pallas_call(
        pack_kernel,
        in_specs=[vmem, vmem],
        out_specs=vmem,
        out_shape=jax.ShapeDtypeStruct((8, 384, 128), BF),
        name="pack",
    )(mine, got)
    groups = [[2 * p + c for p in range(8)] for c in range(2)]
    parts = lax.all_to_all(packed, "op", 0, 0, axis_index_groups=groups, tiled=True)
    sigma, half, gram = pl.pallas_call(
        sum_kernel,
        in_specs=[smem, vmem],
        out_specs=[vmem, vmem, vmem],
        out_shape=[
            jax.ShapeDtypeStruct((32, 512), BF),
            jax.ShapeDtypeStruct((256, 128), F32),
            jax.ShapeDtypeStruct((128, 128), F32),
        ],
        name="gram",
    )(core, parts)
    gram = gram + lax.ppermute(gram, "op", swap)
    rows = lax.dynamic_slice_in_dim(half, (place // 2) * 32, 32, 0)
    lower = jnp.linalg.cholesky(gram)
    basis = math.sqrt(512) * lax.linalg.triangular_solve(
        lower, rows, left_side=False, lower=True, transpose_a=True
    )
    return sigma, basis


def solution(mesh):
    in_specs = (
        P("sec", None, None),
        P("op", "sec", None, None),
        P("op", "sec", None, None),
        P("op"),
        P("sec", None, None),
    )
    out_specs = (P("op", "sec"), P("op", "sec"))
    return jax.shard_map(body, mesh=mesh, in_specs=in_specs, out_specs=out_specs, check_vma=False)
```

```python
import functools
import math

import jax
import jax.numpy as jnp
from jax import lax
from jax.experimental import pallas as pl
from jax.experimental.pallas import tpu as pltpu
from jax.sharding import PartitionSpec as P

BF = jnp.bfloat16
F32 = jnp.float32
EXACT = lax.Precision.HIGHEST
HBM = pl.BlockSpec(memory_space=pltpu.HBM)
VMEM = pl.BlockSpec(memory_space=pltpu.VMEM)
SMEM = pl.BlockSpec(memory_space=pltpu.SMEM)
MIB = 2**20


def call(kernel, name, in_specs, outs, scratch=(), limit=8, flops=1000, bytes_accessed=1000):
    return pl.pallas_call(
        kernel,
        in_specs=in_specs,
        out_specs=[VMEM] * len(outs),
        out_shape=[jax.ShapeDtypeStruct(shape, dtype) for shape, dtype in outs],
        scratch_shapes=scratch,
        compiler_params=pltpu.CompilerParams(vmem_limit_bytes=limit * MIB),
        cost_estimate=pl.CostEstimate(flops=flops, bytes_accessed=bytes_accessed, transcendentals=0),
        name=name,
    )


def load_kernel(left, right, psi, sketch, lout, rout, pout, sout, sems):
    core = lax.axis_index("op") % 2
    copies = [
        pltpu.make_async_copy(psi, pout, sems.at[0]),
        pltpu.make_async_copy(sketch, sout, sems.at[1]),
        pltpu.make_async_copy(left.at[:, :, core], lout.at[:, 0], sems.at[2]),
        pltpu.make_async_copy(left.at[:, :, 1 - core], lout.at[:, 1], sems.at[3]),
        pltpu.make_async_copy(right, rout, sems.at[4]),
    ]
    for copy in copies:
        copy.start()
    for copy in copies:
        copy.wait()


def main_kernel(code, psi, near, far, left, right, sketch, mine, other, inner):
    core = lax.axis_index("op") % 2
    first = jnp.where(core == 0, 2, 0)
    terms = left.shape[0]
    for t in range(terms):
        k = code[t]
        rows = left[t].reshape(512, 512)
        cols = pl.ds(512 * t, 512)

        def times(source):
            inner[:, cols] = jnp.dot(rows, source[...], preferred_element_type=F32).astype(BF)

        pl.when(k == 1)(lambda: times(psi))
        pl.when(k == first)(lambda: times(near))
        pl.when(k == 2 - first)(lambda: times(far))
    scale = 1.0 / math.sqrt(128)
    for h, ref in ((1, other), (0, mine)):
        total = scale * jnp.dot(inner[256 * h : 256 * h + 256, :], right[...], preferred_element_type=F32)
        some = jnp.dot(total.astype(BF), sketch[...], preferred_element_type=F32)
        ref[:, :512] = total.astype(ref.dtype)
        ref[:, 512:] = some.astype(ref.dtype)


def pack_kernel(mine, got, out):
    for p in range(8):
        rows = pl.ds(32 * p, 32)
        for j in range(4):
            cols = pl.ds(128 * j, 128)
            out[p, 32 * j : 32 * j + 32, :] = (mine[rows, cols] + got[rows, cols].astype(F32)).astype(BF)
    some = (mine[:, 512:] + got[:, 512:].astype(F32)).astype(BF)
    for p in range(8):
        out[p, 128:, :] = some


def sum_kernel(got, sigma, half, gram):
    for j in range(4):
        rows = pl.ds(32 * j, 32)
        total = got[0, rows, :].astype(F32)
        for p in range(1, 8):
            total += got[p, rows, :].astype(F32)
        sigma[:, 128 * j : 128 * j + 128] = total.astype(BF)
    total = got[0, 128:, :].astype(F32)
    for p in range(1, 8):
        total += got[p, 128:, :].astype(F32)
    gram[...] = lax.dot_general(
        total, total, (((0,), (0,)), ((), ())), precision=EXACT, preferred_element_type=F32
    )
    half[...] = total


def inverse_rows(a, w, ahead):
    n = len(a)
    row = lax.broadcasted_iota(jnp.int32, (8, 128), 0)
    out = []
    for b in range(n):
        near = range(b, min(b + 1 + ahead, n))
        c = {v: [jnp.broadcast_to(a[v][:, 8 * b + k : 8 * b + k + 1], (8, 128)) for k in range(8)] for v in near}
        scale = jnp.zeros((8, 128), F32)
        for k in range(8):
            s = lax.rsqrt(jnp.broadcast_to(c[b][k][k : k + 1, :], (8, 128)))
            scale = jnp.where(row == k, s, scale)
            f = {v: c[v][k] * (s * s) for v in near}
            f[b] = jnp.where(row > k, f[b], 0.0)
            for m in range(k + 1, 8):
                q = jnp.broadcast_to(c[b][m][k : k + 1, :], (8, 128))
                for v in near:
                    c[v][m] = c[v][m] - f[v] * q
            pa = jnp.broadcast_to(a[b][k : k + 1, :], (8, 128))
            pw = jnp.broadcast_to(w[b][k : k + 1, :], (8, 128))
            for v in near:
                a[v] = a[v] - f[v] * pa
                w[v] = w[v] - f[v] * pw
        u, z = a[b] * scale, w[b] * scale
        out.append(z)
        if b + 1 + ahead < n:
            step = lax.dot_general(
                u, jnp.concatenate([u, z], 1), (((0,), (0,)), ((), ())), precision=EXACT, preferred_element_type=F32
            )
            for v in range(b + 1 + ahead, n):
                a[v] = a[v] - step[8 * v : 8 * v + 8, :128]
                w[v] = w[v] - step[8 * v : 8 * v + 8, 128:]
    return out


def basis_kernel(gram, got, half, basis):
    place = lax.axis_index("op") // 2
    row = lax.broadcasted_iota(jnp.int32, (8, 128), 0)
    lane = lax.broadcasted_iota(jnp.int32, (8, 128), 1)
    a = [gram[8 * v : 8 * v + 8, :] + got[8 * v : 8 * v + 8, :] for v in range(16)]
    w = [jnp.where(lane == row + 8 * v, 1.0, 0.0).astype(F32) for v in range(16)]
    inverse = jnp.concatenate(inverse_rows(a, w, 4), 0)
    rows = half[pl.ds(pl.multiple_of(place * 32, 32), 32), :]
    basis[...] = math.sqrt(512) * lax.dot_general(
        rows, inverse, (((1,), (1,)), ((), ())), precision=EXACT, preferred_element_type=F32
    )


def exchanged(n_op, n_sec):
    pairs = []
    for s in range(n_sec - 1):
        flip = 8 if s == n_sec // 2 - 1 else 0
        for o in range(n_op):
            source, target = (s, s + 1) if o % 2 == 0 else (s + 1, s)
            pairs.append(((o ^ flip) * n_sec + source, o * n_sec + target))
    return pairs


def body(psi, left_env, right_env, pair_code, sketch):
    terms = left_env.shape[0]
    n_op, n_sec = lax.axis_size("op"), lax.axis_size("sec")
    swap = [(i, i ^ 1) for i in range(n_op)]
    near = lax.ppermute(psi[0], ("op", "sec"), exchanged(n_op, n_sec))
    hbm = functools.partial(pltpu.with_memory_space_constraint, memory_space=pltpu.HBM)
    left, right, here, sketch = call(
        load_kernel,
        "load",
        [HBM] * 4,
        [((terms, 2, 8, 32, 512), BF), ((terms * 512, 512), BF), ((512, 512), BF), ((512, 128), BF)],
        [pltpu.SemaphoreType.DMA((5,))],
        limit=1,
        bytes_accessed=18 * MIB,
    )(
        hbm(left_env.reshape(terms, 8, 2, 32, 512)),
        hbm(right_env.reshape(terms * 512, 512)),
        hbm(psi[0]),
        hbm(sketch[0]),
    )
    near, left, right, here, sketch = lax.optimization_barrier((near, left, right, here, sketch))
    far = lax.ppermute(near, "op", swap)
    mine, other = call(
        main_kernel,
        "main",
        [SMEM] + [VMEM] * 6,
        [((256, 640), F32), ((256, 640), BF)],
        [pltpu.VMEM((512, 512 * terms), BF)],
        limit=16,
        flops=4 * 512**3 * terms,
    )(pair_code, here, near, far, left, right, sketch)
    got = lax.ppermute(other, "op", swap)
    (packed,) = call(pack_kernel, "pack", [VMEM] * 2, [((8, 384, 128), BF)])(mine, got)
    groups = [[2 * p + c for p in range(8)] for c in range(2)]
    parts = lax.all_to_all(packed, "op", 0, 0, axis_index_groups=groups, tiled=True)
    sigma, half, gram = call(
        sum_kernel, "gram", [VMEM], [((32, 512), BF), ((256, 128), F32), ((128, 128), F32)]
    )(parts)
    (basis,) = call(basis_kernel, "basis", [VMEM] * 3, [((32, 128), F32)])(
        gram, lax.ppermute(gram, "op", swap), half
    )
    return sigma, basis


def solution(mesh):
    in_specs = (
        P("sec", None, None),
        P("op", "sec", None, None),
        P("op", "sec", None, None),
        P("op"),
        P("sec", None, None),
    )
    out_specs = (P("op", "sec"), P("op", "sec"))
    return jax.shard_map(body, mesh=mesh, in_specs=in_specs, out_specs=out_specs, check_vma=False)
```

```python
import functools
import math

import jax
import jax.numpy as jnp
from jax import lax
from jax.experimental import pallas as pl
from jax.experimental.pallas import tpu as pltpu
from jax.sharding import PartitionSpec as P

BF = jnp.bfloat16
F32 = jnp.float32
EXACT = lax.Precision.HIGHEST
HBM = pl.BlockSpec(memory_space=pltpu.HBM)
VMEM = pl.BlockSpec(memory_space=pltpu.VMEM)
SMEM = pl.BlockSpec(memory_space=pltpu.SMEM)
MIB = 2**20


def call(kernel, name, in_specs, outs, scratch=(), limit=8, flops=1000, bytes_accessed=1000, aliases={}):
    return pl.pallas_call(
        kernel,
        in_specs=in_specs,
        out_specs=[VMEM] * len(outs),
        out_shape=[jax.ShapeDtypeStruct(shape, dtype) for shape, dtype in outs],
        scratch_shapes=scratch,
        input_output_aliases=aliases,
        compiler_params=pltpu.CompilerParams(vmem_limit_bytes=limit * MIB),
        cost_estimate=pl.CostEstimate(flops=flops, bytes_accessed=bytes_accessed, transcendentals=0),
        name=name,
    )


def times(inner, left, t, source):
    rows = left[t].reshape(512, 512)
    inner[:, 512 * t : 512 * t + 512] = jnp.dot(rows, source[...], preferred_element_type=F32).astype(BF)


def load_kernel(code, left, right, psi, sketch, lout, rout, sout, inner, here, sems):
    core = lax.axis_index("op") % 2
    sec, last = lax.axis_index("sec"), lax.axis_size("sec") - 1
    copies = [
        pltpu.make_async_copy(psi, here, sems.at[0]),
        pltpu.make_async_copy(left.at[:, :, core], lout.at[:, 0], sems.at[1]),
        pltpu.make_async_copy(left.at[:, :, 1 - core], lout.at[:, 1], sems.at[2]),
        pltpu.make_async_copy(right, rout, sems.at[3]),
        pltpu.make_async_copy(sketch, sout, sems.at[4]),
    ]
    for copy in copies:
        copy.start()
    for copy in copies[:3]:
        copy.wait()
    for t in range(left.shape[0]):
        k = code[t]

        @pl.when(k == 1)
        def _():
            times(inner, lout, t, here)

        @pl.when(((k == 2) & (sec == 0)) | ((k == 0) & (sec == last)))
        def _():
            inner[:, 512 * t : 512 * t + 512] = jnp.zeros((512, 512), BF)

    for copy in copies[3:]:
        copy.wait()


def multiply(code, inner, left, source, wanted):
    sec, last = lax.axis_index("sec"), lax.axis_size("sec") - 1
    for t in range(left.shape[0]):
        k = code[t]
        empty = ((k == 2) & (sec == 0)) | ((k == 0) & (sec == last))

        @pl.when((k == wanted) & jnp.logical_not(empty))
        def _():
            times(inner, left, t, source)


def near_kernel(code, near, left, before, inner):
    core = lax.axis_index("op") % 2
    multiply(code, inner, left, near, jnp.where(core == 0, 2, 0))


def finish(inner, right, sketch, h, ref):
    total = jnp.dot(inner[256 * h : 256 * h + 256, :], right[...], preferred_element_type=F32)
    total = total * (1.0 / math.sqrt(128))
    ref[:, :512] = total.astype(ref.dtype)
    ref[:, 512:] = jnp.dot(total.astype(BF), sketch[...], preferred_element_type=F32).astype(ref.dtype)


def far_kernel(code, far, left, right, sketch, before, inner, other):
    core = lax.axis_index("op") % 2
    multiply(code, inner, left, far, jnp.where(core == 0, 0, 2))
    finish(inner, right, sketch, 1, other)


def mine_kernel(inner, right, sketch, mine):
    finish(inner, right, sketch, 0, mine)


def pack_kernel(mine, got, out):
    for p in range(8):
        rows = pl.ds(32 * p, 32)
        for j in range(4):
            cols = pl.ds(128 * j, 128)
            out[p, 32 * j : 32 * j + 32, :] = (mine[rows, cols] + got[rows, cols].astype(F32)).astype(BF)
    some = (mine[:, 512:] + got[:, 512:].astype(F32)).astype(BF)
    for p in range(8):
        out[p, 128:, :] = some


def sum_kernel(got, sigma, half, gram):
    for j in range(4):
        rows = pl.ds(32 * j, 32)
        total = got[0, rows, :].astype(F32)
        for p in range(1, 8):
            total += got[p, rows, :].astype(F32)
        sigma[:, 128 * j : 128 * j + 128] = total.astype(BF)
    total = got[0, 128:, :].astype(F32)
    for p in range(1, 8):
        total += got[p, 128:, :].astype(F32)
    gram[...] = lax.dot_general(
        total, total, (((0,), (0,)), ((), ())), precision=EXACT, preferred_element_type=F32
    )
    half[...] = total


def inverse_rows(a, w, ahead):
    n = len(a)
    row = lax.broadcasted_iota(jnp.int32, (8, 128), 0)
    out = []
    for b in range(n):
        near = range(b, min(b + 1 + ahead, n))
        c = {v: [jnp.broadcast_to(a[v][:, 8 * b + k : 8 * b + k + 1], (8, 128)) for k in range(8)] for v in near}
        scale = jnp.zeros((8, 128), F32)
        for k in range(8):
            s = lax.rsqrt(jnp.broadcast_to(c[b][k][k : k + 1, :], (8, 128)))
            scale = jnp.where(row == k, s, scale)
            f = {v: c[v][k] * (s * s) for v in near}
            f[b] = jnp.where(row > k, f[b], 0.0)
            for m in range(k + 1, 8):
                q = jnp.broadcast_to(c[b][m][k : k + 1, :], (8, 128))
                for v in near:
                    c[v][m] = c[v][m] - f[v] * q
            pa = jnp.broadcast_to(a[b][k : k + 1, :], (8, 128))
            pw = jnp.broadcast_to(w[b][k : k + 1, :], (8, 128))
            for v in near:
                a[v] = a[v] - f[v] * pa
                w[v] = w[v] - f[v] * pw
        u, z = a[b] * scale, w[b] * scale
        out.append(z)
        if b + 1 + ahead < n:
            step = lax.dot_general(
                u, jnp.concatenate([u, z], 1), (((0,), (0,)), ((), ())), precision=EXACT, preferred_element_type=F32
            )
            for v in range(b + 1 + ahead, n):
                a[v] = a[v] - step[8 * v : 8 * v + 8, :128]
                w[v] = w[v] - step[8 * v : 8 * v + 8, 128:]
    return out


def basis_kernel(gram, got, half, basis):
    place = lax.axis_index("op") // 2
    row = lax.broadcasted_iota(jnp.int32, (8, 128), 0)
    lane = lax.broadcasted_iota(jnp.int32, (8, 128), 1)
    a = [gram[8 * v : 8 * v + 8, :] + got[8 * v : 8 * v + 8, :] for v in range(16)]
    w = [jnp.where(lane == row + 8 * v, 1.0, 0.0).astype(F32) for v in range(16)]
    inverse = jnp.concatenate(inverse_rows(a, w, 4), 0)
    rows = half[pl.ds(pl.multiple_of(place * 32, 32), 32), :]
    basis[...] = math.sqrt(512) * lax.dot_general(
        rows, inverse, (((1,), (1,)), ((), ())), precision=EXACT, preferred_element_type=F32
    )


def exchanged(n_op, n_sec):
    pairs = []
    for s in range(n_sec - 1):
        flip = 8 if s == n_sec // 2 - 1 else 0
        for o in range(n_op):
            source, target = (s, s + 1) if o % 2 == 0 else (s + 1, s)
            pairs.append(((o ^ flip) * n_sec + source, o * n_sec + target))
    for o in range(0, n_op, 2):
        pairs.append((o * n_sec + n_sec - 1, (o + 1) * n_sec + n_sec - 1))
        pairs.append(((o + 1) * n_sec, o * n_sec))
    return pairs


def body(psi, left_env, right_env, pair_code, sketch):
    terms = left_env.shape[0]
    n_op, n_sec = lax.axis_size("op"), lax.axis_size("sec")
    swap = [(i, i ^ 1) for i in range(n_op)]
    near = lax.ppermute(psi[0], ("op", "sec"), exchanged(n_op, n_sec))
    hbm = functools.partial(pltpu.with_memory_space_constraint, memory_space=pltpu.HBM)
    products = ((512, 512 * terms), BF)
    left, right, sketch, inner = call(
        load_kernel,
        "load",
        [SMEM] + [HBM] * 4,
        [((terms, 2, 8, 32, 512), BF), ((terms * 512, 512), BF), ((512, 128), BF), products],
        [pltpu.VMEM((512, 512), BF), pltpu.SemaphoreType.DMA((5,))],
        limit=4,
        bytes_accessed=18 * MIB,
    )(
        pair_code,
        hbm(left_env.reshape(terms, 8, 2, 32, 512)),
        hbm(right_env.reshape(terms * 512, 512)),
        hbm(psi[0]),
        hbm(sketch[0]),
    )
    near, left, right, sketch, inner = lax.optimization_barrier((near, left, right, sketch, inner))
    far = lax.ppermute(near, "op", swap)
    flops = 2 * 512**3 * terms
    (inner,) = call(
        near_kernel, "near", [SMEM] + [VMEM] * 3, [products], limit=4, flops=flops // 3, aliases={3: 0}
    )(pair_code, near, left, inner)
    inner, other = call(
        far_kernel,
        "far",
        [SMEM] + [VMEM] * 5,
        [products, ((256, 640), BF)],
        limit=6,
        flops=flops,
        aliases={5: 0},
    )(pair_code, far, left, right, sketch, inner)
    got = lax.ppermute(other, "op", swap)
    (mine,) = call(mine_kernel, "mine", [VMEM] * 3, [((256, 640), F32)], limit=6, flops=flops // 2)(
        inner, right, sketch
    )
    (packed,) = call(pack_kernel, "pack", [VMEM] * 2, [((8, 384, 128), BF)])(mine, got)
    groups = [[2 * p + c for p in range(8)] for c in range(2)]
    parts = lax.all_to_all(packed, "op", 0, 0, axis_index_groups=groups, tiled=True)
    sigma, half, gram = call(
        sum_kernel, "gram", [VMEM], [((32, 512), BF), ((256, 128), F32), ((128, 128), F32)]
    )(parts)
    (basis,) = call(basis_kernel, "basis", [VMEM] * 3, [((32, 128), F32)])(
        gram, lax.ppermute(gram, "op", swap), half
    )
    return sigma, basis


def solution(mesh):
    in_specs = (
        P("sec", None, None),
        P("op", "sec", None, None),
        P("op", "sec", None, None),
        P("op"),
        P("sec", None, None),
    )
    out_specs = (P("op", "sec"), P("op", "sec"))
    return jax.shard_map(body, mesh=mesh, in_specs=in_specs, out_specs=out_specs, check_vma=False)
```

```python
import functools
import math

import jax
import jax.numpy as jnp
from jax import lax
from jax.experimental import pallas as pl
from jax.experimental.pallas import tpu as pltpu
from jax.sharding import PartitionSpec as P

BF = jnp.bfloat16
F32 = jnp.float32
EXACT = lax.Precision.HIGHEST
HBM = pl.BlockSpec(memory_space=pltpu.HBM)
VMEM = pl.BlockSpec(memory_space=pltpu.VMEM)
SMEM = pl.BlockSpec(memory_space=pltpu.SMEM)
MIB = 2**20


def call(kernel, name, in_specs, outs, scratch=(), limit=8, flops=1000, bytes_accessed=1000, aliases={}):
    return pl.pallas_call(
        kernel,
        in_specs=in_specs,
        out_specs=[VMEM] * len(outs),
        out_shape=[jax.ShapeDtypeStruct(shape, dtype) for shape, dtype in outs],
        scratch_shapes=scratch,
        input_output_aliases=aliases,
        compiler_params=pltpu.CompilerParams(vmem_limit_bytes=limit * MIB),
        cost_estimate=pl.CostEstimate(flops=flops, bytes_accessed=bytes_accessed, transcendentals=0),
        name=name,
    )


def times(inner, left, t, source):
    rows = left[t].reshape(512, 512)
    inner[:, 512 * t : 512 * t + 512] = jnp.dot(rows, source[...], preferred_element_type=F32).astype(BF)


def load_kernel(code, left, right, psi, sketch, lout, rout, sout, inner, here, sems):
    core = lax.axis_index("op") % 2
    sec, last = lax.axis_index("sec"), lax.axis_size("sec") - 1
    copies = [
        pltpu.make_async_copy(psi, here, sems.at[0]),
        pltpu.make_async_copy(left.at[:, :, core], lout.at[:, 0], sems.at[1]),
        pltpu.make_async_copy(left.at[:, :, 1 - core], lout.at[:, 1], sems.at[2]),
        pltpu.make_async_copy(right, rout, sems.at[3]),
        pltpu.make_async_copy(sketch, sout, sems.at[4]),
    ]
    for copy in copies:
        copy.start()
    for copy in copies[:3]:
        copy.wait()
    for t in range(left.shape[0]):
        k = code[t]

        @pl.when(k == 1)
        def _():
            times(inner, lout, t, here)

        @pl.when(((k == 2) & (sec == 0)) | ((k == 0) & (sec == last)))
        def _():
            inner[:, 512 * t : 512 * t + 512] = jnp.zeros((512, 512), BF)

    for copy in copies[3:]:
        copy.wait()


def multiply(code, inner, left, source, wanted):
    sec, last = lax.axis_index("sec"), lax.axis_size("sec") - 1
    for t in range(left.shape[0]):
        k = code[t]
        empty = ((k == 2) & (sec == 0)) | ((k == 0) & (sec == last))

        @pl.when((k == wanted) & jnp.logical_not(empty))
        def _():
            times(inner, left, t, source)


def near_kernel(code, near, left, before, inner):
    core = lax.axis_index("op") % 2
    multiply(code, inner, left, near, jnp.where(core == 0, 2, 0))


def finish(inner, right, sketch, h, ref):
    total = jnp.dot(inner[256 * h : 256 * h + 256, :], right[...], preferred_element_type=F32)
    total = total * (1.0 / math.sqrt(128))
    ref[:, :512] = total.astype(ref.dtype)
    ref[:, 512:] = jnp.dot(total.astype(BF), sketch[...], preferred_element_type=F32).astype(ref.dtype)


def far_kernel(code, far, left, right, sketch, before, inner, other):
    core = lax.axis_index("op") % 2
    multiply(code, inner, left, far, jnp.where(core == 0, 0, 2))
    finish(inner, right, sketch, 1, other)


def mine_kernel(inner, right, sketch, mine):
    finish(inner, right, sketch, 0, mine)


def pack_kernel(mine, got, out):
    for p in range(8):
        rows = pl.ds(32 * p, 32)
        for j in range(4):
            cols = pl.ds(128 * j, 128)
            out[p, 32 * j : 32 * j + 32, :] = (mine[rows, cols] + got[rows, cols].astype(F32)).astype(BF)
    some = (mine[:, 512:] + got[:, 512:].astype(F32)).astype(BF)
    for p in range(8):
        out[p, 128:, :] = some


def sum_kernel(got, sigma, half, gram):
    for j in range(4):
        rows = pl.ds(32 * j, 32)
        total = got[0, rows, :].astype(F32)
        for p in range(1, 8):
            total += got[p, rows, :].astype(F32)
        sigma[:, 128 * j : 128 * j + 128] = total.astype(BF)
    total = got[0, 128:, :].astype(F32)
    for p in range(1, 8):
        total += got[p, 128:, :].astype(F32)
    gram[...] = lax.dot_general(
        total, total, (((0,), (0,)), ((), ())), precision=EXACT, preferred_element_type=F32
    )
    half[...] = total


def inverse_rows(m, ahead):
    n = len(m)
    row = lax.broadcasted_iota(jnp.int32, (8, 128), 0)
    lane = lax.broadcasted_iota(jnp.int32, (8, 128), 1)
    out = []
    for b in range(n):
        near = range(b, min(b + 1 + ahead, n))
        c = {v: [jnp.broadcast_to(m[v][:, 8 * b + k : 8 * b + k + 1], (8, 128)) for k in range(8)] for v in near}
        here = (lane >= 8 * b) & (lane < 8 * b + 8)
        for v in range(b, n):
            m[v] = jnp.where(here, jnp.where(lane == row + 8 * b, 1.0, 0.0) if v == b else 0.0, m[v])
        scale = jnp.zeros((8, 128), F32)
        for k in range(8):
            s = lax.rsqrt(jnp.broadcast_to(c[b][k][k : k + 1, :], (8, 128)))
            scale = jnp.where(row == k, s, scale)
            f = {v: c[v][k] * (s * s) for v in near}
            f[b] = jnp.where(row > k, f[b], 0.0)
            for j in range(k + 1, 8):
                q = jnp.broadcast_to(c[b][j][k : k + 1, :], (8, 128))
                for v in near:
                    c[v][j] = c[v][j] - f[v] * q
            pivot = jnp.broadcast_to(m[b][k : k + 1, :], (8, 128))
            for v in near:
                m[v] = m[v] - f[v] * pivot
        u = m[b] * scale
        out.append(jnp.where(lane < 8 * b + 8, u, 0.0))
        if b + 1 + ahead < n:
            step = lax.dot_general(u, u, (((0,), (0,)), ((), ())), precision=EXACT, preferred_element_type=F32)
            for v in range(b + 1 + ahead, n):
                m[v] = m[v] - step[8 * v : 8 * v + 8]
    return out


def basis_kernel(gram, got, half, basis):
    place = lax.axis_index("op") // 2
    m = [gram[8 * v : 8 * v + 8, :] + got[8 * v : 8 * v + 8, :] for v in range(16)]
    inverse = jnp.concatenate(inverse_rows(m, 3), 0)
    rows = half[pl.ds(pl.multiple_of(place * 32, 32), 32), :]
    basis[...] = math.sqrt(512) * lax.dot_general(
        rows, inverse, (((1,), (1,)), ((), ())), precision=EXACT, preferred_element_type=F32
    )


def exchanged(n_op, n_sec):
    pairs = []
    for s in range(n_sec - 1):
        flip = 8 if s == n_sec // 2 - 1 else 0
        for o in range(0, n_op, 2):
            up = o if s == 0 else o + 1
            down = o + 1 if s == n_sec - 2 else o
            pairs.append(((up ^ flip) * n_sec + s, o * n_sec + s + 1))
            pairs.append((down * n_sec + s + 1, ((o + 1) ^ flip) * n_sec + s))
    for o in range(0, n_op, 2):
        pairs.append(((o + 1) * n_sec, o * n_sec))
        pairs.append((o * n_sec + n_sec - 1, (o + 1) * n_sec + n_sec - 1))
    return pairs


def body(psi, left_env, right_env, pair_code, sketch):
    terms = left_env.shape[0]
    n_op, n_sec = lax.axis_size("op"), lax.axis_size("sec")
    swap = [(i, i ^ 1) for i in range(n_op)]
    near = lax.ppermute(psi[0], ("op", "sec"), exchanged(n_op, n_sec))
    hbm = functools.partial(pltpu.with_memory_space_constraint, memory_space=pltpu.HBM)
    products = ((512, 512 * terms), BF)
    left, right, sketch, inner = call(
        load_kernel,
        "load",
        [SMEM] + [HBM] * 4,
        [((terms, 2, 8, 32, 512), BF), ((terms * 512, 512), BF), ((512, 128), BF), products],
        [pltpu.VMEM((512, 512), BF), pltpu.SemaphoreType.DMA((5,))],
        limit=4,
        bytes_accessed=18 * MIB,
    )(
        pair_code,
        hbm(left_env.reshape(terms, 8, 2, 32, 512)),
        hbm(right_env.reshape(terms * 512, 512)),
        hbm(psi[0]),
        hbm(sketch[0]),
    )
    near, left, right, sketch, inner = lax.optimization_barrier((near, left, right, sketch, inner))
    far = lax.ppermute(near, "op", swap)
    flops = 2 * 512**3 * terms
    (inner,) = call(
        near_kernel, "near", [SMEM] + [VMEM] * 3, [products], limit=4, flops=flops // 3, aliases={3: 0}
    )(pair_code, near, left, inner)
    inner, other = call(
        far_kernel,
        "far",
        [SMEM] + [VMEM] * 5,
        [products, ((256, 640), BF)],
        limit=6,
        flops=flops,
        aliases={5: 0},
    )(pair_code, far, left, right, sketch, inner)
    got = lax.ppermute(other, "op", swap)
    (mine,) = call(mine_kernel, "mine", [VMEM] * 3, [((256, 640), F32)], limit=6, flops=flops // 2)(
        inner, right, sketch
    )
    (packed,) = call(pack_kernel, "pack", [VMEM] * 2, [((8, 384, 128), BF)])(mine, got)
    groups = [[2 * p + c for p in range(8)] for c in range(2)]
    parts = lax.all_to_all(packed, "op", 0, 0, axis_index_groups=groups, tiled=True)
    sigma, half, gram = call(
        sum_kernel, "gram", [VMEM], [((32, 512), BF), ((256, 128), F32), ((128, 128), F32)]
    )(parts)
    (basis,) = call(basis_kernel, "basis", [VMEM] * 3, [((32, 128), F32)])(
        gram, lax.ppermute(gram, "op", swap), half
    )
    return sigma, basis


def solution(mesh):
    in_specs = (
        P("sec", None, None),
        P("op", "sec", None, None),
        P("op", "sec", None, None),
        P("op"),
        P("sec", None, None),
    )
    out_specs = (P("op", "sec"), P("op", "sec"))
    return jax.shard_map(body, mesh=mesh, in_specs=in_specs, out_specs=out_specs, check_vma=False)
```

```python
import functools
import math

import jax
import jax.numpy as jnp
from jax import lax
from jax.experimental import pallas as pl
from jax.experimental.pallas import tpu as pltpu
from jax.sharding import PartitionSpec as P

BF = jnp.bfloat16
F32 = jnp.float32
EXACT = lax.Precision.HIGHEST
HBM = pl.BlockSpec(memory_space=pltpu.HBM)
VMEM = pl.BlockSpec(memory_space=pltpu.VMEM)
SMEM = pl.BlockSpec(memory_space=pltpu.SMEM)
MIB = 2**20
CHIPS = (0, 4, 5, 1, 2, 6, 7, 3)


def call(kernel, name, in_specs, outs, scratch=(), limit=8, flops=1000, bytes_accessed=1000, aliases={}):
    return pl.pallas_call(
        kernel,
        in_specs=in_specs,
        out_specs=[VMEM] * len(outs),
        out_shape=[jax.ShapeDtypeStruct(shape, dtype) for shape, dtype in outs],
        scratch_shapes=scratch,
        input_output_aliases=aliases,
        compiler_params=pltpu.CompilerParams(vmem_limit_bytes=limit * MIB),
        cost_estimate=pl.CostEstimate(flops=flops, bytes_accessed=bytes_accessed, transcendentals=0),
        name=name,
    )


def times(inner, left, t, source):
    rows = left[t].reshape(512, 512)
    inner[:, 512 * t : 512 * t + 512] = jnp.dot(rows, source[...], preferred_element_type=F32).astype(BF)


def load_kernel(code, left, right, psi, sketch, lout, rout, sout, inner, here, sems):
    core = lax.axis_index("op") % 2
    sec, last = lax.axis_index("sec"), lax.axis_size("sec") - 1
    copies = [
        pltpu.make_async_copy(psi, here, sems.at[0]),
        pltpu.make_async_copy(left.at[:, :, core], lout.at[:, 0], sems.at[1]),
        pltpu.make_async_copy(left.at[:, :, 1 - core], lout.at[:, 1], sems.at[2]),
        pltpu.make_async_copy(right, rout, sems.at[3]),
        pltpu.make_async_copy(sketch, sout, sems.at[4]),
    ]
    for copy in copies:
        copy.start()
    for copy in copies[:3]:
        copy.wait()
    for t in range(left.shape[0]):
        k = code[t]

        @pl.when(k == 1)
        def _():
            times(inner, lout, t, here)

        @pl.when(((k == 2) & (sec == 0)) | ((k == 0) & (sec == last)))
        def _():
            inner[:, 512 * t : 512 * t + 512] = jnp.zeros((512, 512), BF)

    for copy in copies[3:]:
        copy.wait()


def multiply(code, inner, left, source, wanted):
    sec, last = lax.axis_index("sec"), lax.axis_size("sec") - 1
    for t in range(left.shape[0]):
        k = code[t]
        empty = ((k == 2) & (sec == 0)) | ((k == 0) & (sec == last))

        @pl.when((k == wanted) & jnp.logical_not(empty))
        def _():
            times(inner, left, t, source)


def near_kernel(code, near, left, before, inner):
    core = lax.axis_index("op") % 2
    multiply(code, inner, left, near, jnp.where(core == 0, 2, 0))


def finish(inner, right, sketch, h, ref):
    total = jnp.dot(inner[256 * h : 256 * h + 256, :], right[...], preferred_element_type=F32)
    total = total * (1.0 / math.sqrt(128))
    ref[:, :512] = total.astype(ref.dtype)
    ref[:, 512:] = jnp.dot(total.astype(BF), sketch[...], preferred_element_type=F32).astype(ref.dtype)


def far_kernel(code, far, left, right, sketch, before, inner, other):
    core = lax.axis_index("op") % 2
    multiply(code, inner, left, far, jnp.where(core == 0, 0, 2))
    finish(inner, right, sketch, 1, other)


def mine_kernel(inner, right, sketch, mine):
    finish(inner, right, sketch, 0, mine)


def pack_kernel(mine, got, out):
    for i, p in enumerate(CHIPS):
        rows = pl.ds(32 * p, 32)
        for j in range(4):
            cols = pl.ds(128 * j, 128)
            out[i, 32 * j : 32 * j + 32, :] = (mine[rows, cols] + got[rows, cols].astype(F32)).astype(BF)
    some = (mine[:, 512:] + got[:, 512:].astype(F32)).astype(BF)
    for i in range(8):
        out[i, 128:, :] = some


def sum_kernel(got, sigma, half, gram):
    for j in range(4):
        rows = pl.ds(32 * j, 32)
        total = got[0, rows, :].astype(F32)
        for p in range(1, 8):
            total += got[p, rows, :].astype(F32)
        sigma[:, 128 * j : 128 * j + 128] = total.astype(BF)
    total = got[0, 128:, :].astype(F32)
    for p in range(1, 8):
        total += got[p, 128:, :].astype(F32)
    gram[...] = lax.dot_general(
        total, total, (((0,), (0,)), ((), ())), precision=EXACT, preferred_element_type=F32
    )
    half[...] = total


def inverse_rows(m, window, ahead):
    n, size = len(m), 8 * window
    row = lax.broadcasted_iota(jnp.int32, (8, 128), 0)
    lane = lax.broadcasted_iota(jnp.int32, (8, 128), 1)
    out = []
    for b in range(0, n, window):
        top, near, base = range(b, b + window), range(b, min(b + window + ahead, n)), 8 * b
        c = {v: [jnp.broadcast_to(m[v][:, base + k : base + k + 1], (8, 128)) for k in range(size)] for v in near}
        here = (lane >= base) & (lane < base + size)
        for v in range(b, n):
            m[v] = jnp.where(here, jnp.where(lane == row + 8 * v, 1.0, 0.0) if v in top else 0.0, m[v])
        scale = {v: jnp.zeros((8, 128), F32) for v in top}
        for k in range(size):
            h, i = b + k // 8, k % 8
            s = lax.rsqrt(jnp.broadcast_to(c[h][k][i : i + 1, :], (8, 128)))
            scale[h] = jnp.where(row == i, s, scale[h])
            below = [v for v in near if v >= h]
            f = {v: c[v][k] * (s * s) for v in below}
            f[h] = jnp.where(row > i, f[h], 0.0)
            for j in range(k + 1, size):
                q = jnp.broadcast_to(c[h][j][i : i + 1, :], (8, 128))
                for v in below:
                    c[v][j] = c[v][j] - f[v] * q
            pivot = jnp.broadcast_to(m[h][i : i + 1, :], (8, 128))
            for v in below:
                m[v] = m[v] - f[v] * pivot
        done = [m[v] * scale[v] for v in top]
        out += [jnp.where(lane < 8 * v + 8, u, 0.0) for v, u in zip(top, done)]
        if b + window + ahead < n:
            u = jnp.concatenate(done, 0)
            step = lax.dot_general(u, u, (((0,), (0,)), ((), ())), precision=EXACT, preferred_element_type=F32)
            for v in range(b + window + ahead, n):
                m[v] = m[v] - step[8 * v : 8 * v + 8]
    return out


def basis_kernel(gram, got, half, basis):
    place = lax.axis_index("op") // 2
    m = [gram[8 * v : 8 * v + 8, :] + got[8 * v : 8 * v + 8, :] for v in range(16)]
    inverse = jnp.concatenate(inverse_rows(m, 2, 2), 0)
    rows = half[pl.ds(pl.multiple_of(place * 32, 32), 32), :]
    basis[...] = math.sqrt(512) * lax.dot_general(
        rows, inverse, (((1,), (1,)), ((), ())), precision=EXACT, preferred_element_type=F32
    )


def exchanged(n_op, n_sec):
    pairs = []
    for s in range(n_sec - 1):
        flip = 8 if s == n_sec // 2 - 1 else 0
        for o in range(0, n_op, 2):
            up = o if s == 0 else o + 1
            down = o + 1 if s == n_sec - 2 else o
            pairs.append(((up ^ flip) * n_sec + s, o * n_sec + s + 1))
            pairs.append((down * n_sec + s + 1, ((o + 1) ^ flip) * n_sec + s))
    for o in range(0, n_op, 2):
        pairs.append(((o + 1) * n_sec, o * n_sec))
        pairs.append((o * n_sec + n_sec - 1, (o + 1) * n_sec + n_sec - 1))
    return pairs


def body(psi, left_env, right_env, pair_code, sketch):
    terms = left_env.shape[0]
    n_op, n_sec = lax.axis_size("op"), lax.axis_size("sec")
    swap = [(i, i ^ 1) for i in range(n_op)]
    near = lax.ppermute(psi[0], ("op", "sec"), exchanged(n_op, n_sec))
    hbm = functools.partial(pltpu.with_memory_space_constraint, memory_space=pltpu.HBM)
    products = ((512, 512 * terms), BF)
    left, right, sketch, inner = call(
        load_kernel,
        "load",
        [SMEM] + [HBM] * 4,
        [((terms, 2, 8, 32, 512), BF), ((terms * 512, 512), BF), ((512, 128), BF), products],
        [pltpu.VMEM((512, 512), BF), pltpu.SemaphoreType.DMA((5,))],
        limit=4,
        bytes_accessed=18 * MIB,
    )(
        pair_code,
        hbm(left_env.reshape(terms, 8, 2, 32, 512)),
        hbm(right_env.reshape(terms * 512, 512)),
        hbm(psi[0]),
        hbm(sketch[0]),
    )
    near, left, right, sketch, inner = lax.optimization_barrier((near, left, right, sketch, inner))
    far = lax.ppermute(near, "op", swap)
    flops = 2 * 512**3 * terms
    (inner,) = call(
        near_kernel, "near", [SMEM] + [VMEM] * 3, [products], limit=4, flops=flops // 3, aliases={3: 0}
    )(pair_code, near, left, inner)
    inner, other = call(
        far_kernel,
        "far",
        [SMEM] + [VMEM] * 5,
        [products, ((256, 640), BF)],
        limit=6,
        flops=flops,
        aliases={5: 0},
    )(pair_code, far, left, right, sketch, inner)
    got = lax.ppermute(other, "op", swap)
    (mine,) = call(mine_kernel, "mine", [VMEM] * 3, [((256, 640), F32)], limit=6, flops=flops // 2)(
        inner, right, sketch
    )
    (packed,) = call(pack_kernel, "pack", [VMEM] * 2, [((8, 384, 128), BF)])(mine, got)
    groups = [[2 * p + c for p in CHIPS] for c in range(2)]
    parts = lax.all_to_all(packed, "op", 0, 0, axis_index_groups=groups, tiled=True)
    sigma, half, gram = call(
        sum_kernel, "gram", [VMEM], [((32, 512), BF), ((256, 128), F32), ((128, 128), F32)]
    )(parts)
    (basis,) = call(basis_kernel, "basis", [VMEM] * 3, [((32, 128), F32)])(
        gram, lax.ppermute(gram, "op", swap), half
    )
    return sigma, basis


def solution(mesh):
    in_specs = (
        P("sec", None, None),
        P("op", "sec", None, None),
        P("op", "sec", None, None),
        P("op"),
        P("sec", None, None),
    )
    out_specs = (P("op", "sec"), P("op", "sec"))
    return jax.shard_map(body, mesh=mesh, in_specs=in_specs, out_specs=out_specs, check_vma=False)
```

```python
import functools
import math

import jax
import jax.numpy as jnp
from jax import lax
from jax.experimental import pallas as pl
from jax.experimental.pallas import tpu as pltpu
from jax.sharding import PartitionSpec as P

BF = jnp.bfloat16
F32 = jnp.float32
EXACT = lax.Precision.HIGHEST
HBM = pl.BlockSpec(memory_space=pltpu.HBM)
VMEM = pl.BlockSpec(memory_space=pltpu.VMEM)
SMEM = pl.BlockSpec(memory_space=pltpu.SMEM)
MIB = 2**20
CHIPS = (0, 4, 5, 1, 2, 6, 7, 3)


def call(kernel, name, in_specs, outs, scratch=(), limit=8, flops=1000, bytes_accessed=1000, aliases={}):
    return pl.pallas_call(
        kernel,
        in_specs=in_specs,
        out_specs=[VMEM] * len(outs),
        out_shape=[jax.ShapeDtypeStruct(shape, dtype) for shape, dtype in outs],
        scratch_shapes=scratch,
        input_output_aliases=aliases,
        compiler_params=pltpu.CompilerParams(vmem_limit_bytes=limit * MIB),
        cost_estimate=pl.CostEstimate(flops=flops, bytes_accessed=bytes_accessed, transcendentals=0),
        name=name,
    )


def times(inner, left, t, source):
    rows = left[t].reshape(512, 512)
    inner[:, 512 * t : 512 * t + 512] = jnp.dot(rows, source[...], preferred_element_type=F32).astype(BF)


def load_kernel(code, left, right, psi, sketch, lout, rout, sout, inner, here, sems):
    core = lax.axis_index("op") % 2
    sec, last = lax.axis_index("sec"), lax.axis_size("sec") - 1
    copies = [
        pltpu.make_async_copy(psi, here, sems.at[0]),
        pltpu.make_async_copy(left.at[:, :, core], lout.at[:, 0], sems.at[1]),
        pltpu.make_async_copy(left.at[:, :, 1 - core], lout.at[:, 1], sems.at[2]),
        pltpu.make_async_copy(right, rout, sems.at[3]),
        pltpu.make_async_copy(sketch, sout, sems.at[4]),
    ]
    for copy in copies:
        copy.start()
    for copy in copies[:3]:
        copy.wait()
    for t in range(left.shape[0]):
        k = code[t]

        @pl.when(k == 1)
        def _():
            times(inner, lout, t, here)

        @pl.when(((k == 2) & (sec == 0)) | ((k == 0) & (sec == last)))
        def _():
            inner[:, 512 * t : 512 * t + 512] = jnp.zeros((512, 512), BF)

    for copy in copies[3:]:
        copy.wait()


def multiply(code, inner, left, source, wanted):
    sec, last = lax.axis_index("sec"), lax.axis_size("sec") - 1
    for t in range(left.shape[0]):
        k = code[t]
        empty = ((k == 2) & (sec == 0)) | ((k == 0) & (sec == last))

        @pl.when((k == wanted) & jnp.logical_not(empty))
        def _():
            times(inner, left, t, source)


def near_kernel(code, near, left, before, inner):
    core = lax.axis_index("op") % 2
    multiply(code, inner, left, near, jnp.where(core == 0, 2, 0))


def finish(inner, right, sketch, h, ref):
    total = jnp.dot(inner[256 * h : 256 * h + 256, :], right[...], preferred_element_type=F32)
    total = total * (1.0 / math.sqrt(128))
    ref[:, :512] = total.astype(ref.dtype)
    ref[:, 512:] = jnp.dot(total.astype(BF), sketch[...], preferred_element_type=F32).astype(ref.dtype)


def far_kernel(code, far, left, right, sketch, before, inner, other):
    core = lax.axis_index("op") % 2
    multiply(code, inner, left, far, jnp.where(core == 0, 0, 2))
    finish(inner, right, sketch, 1, other)


def mine_kernel(inner, right, sketch, mine):
    finish(inner, right, sketch, 0, mine)


def pack_kernel(mine, got, out):
    for i, p in enumerate(CHIPS):
        rows = pl.ds(32 * p, 32)
        for j in range(4):
            cols = pl.ds(128 * j, 128)
            out[i, 32 * j : 32 * j + 32, :] = (mine[rows, cols] + got[rows, cols].astype(F32)).astype(BF)
    some = (mine[:, 512:] + got[:, 512:].astype(F32)).astype(BF)
    for i in range(8):
        out[i, 128:, :] = some


def sum_kernel(got, half, gram):
    total = got[0, 128:, :].astype(F32)
    for p in range(1, 8):
        total += got[p, 128:, :].astype(F32)
    gram[...] = lax.dot_general(
        total, total, (((0,), (0,)), ((), ())), precision=EXACT, preferred_element_type=F32
    )
    half[...] = total


def sigma_kernel(got, sigma):
    for j in range(4):
        rows = pl.ds(32 * j, 32)
        total = got[0, rows, :].astype(F32)
        for p in range(1, 8):
            total += got[p, rows, :].astype(F32)
        sigma[:, 128 * j : 128 * j + 128] = total.astype(BF)


def inverse_rows(m, window, ahead):
    n, size = len(m), 8 * window
    row = lax.broadcasted_iota(jnp.int32, (8, 128), 0)
    lane = lax.broadcasted_iota(jnp.int32, (8, 128), 1)
    out = []
    for b in range(0, n, window):
        top, near, base = range(b, b + window), range(b, min(b + window + ahead, n)), 8 * b
        c = {v: [jnp.broadcast_to(m[v][:, base + k : base + k + 1], (8, 128)) for k in range(size)] for v in near}
        here = (lane >= base) & (lane < base + size)
        for v in range(b, n):
            m[v] = jnp.where(here, jnp.where(lane == row + 8 * v, 1.0, 0.0) if v in top else 0.0, m[v])
        scale = {v: jnp.zeros((8, 128), F32) for v in top}
        for k in range(size):
            h, i = b + k // 8, k % 8
            s = lax.rsqrt(jnp.broadcast_to(c[h][k][i : i + 1, :], (8, 128)))
            scale[h] = jnp.where(row == i, s, scale[h])
            below = [v for v in near if v >= h]
            f = {v: c[v][k] * (s * s) for v in below}
            f[h] = jnp.where(row > i, f[h], 0.0)
            for j in range(k + 1, size):
                q = jnp.broadcast_to(c[h][j][i : i + 1, :], (8, 128))
                for v in below:
                    c[v][j] = c[v][j] - f[v] * q
            pivot = jnp.broadcast_to(m[h][i : i + 1, :], (8, 128))
            for v in below:
                m[v] = m[v] - f[v] * pivot
        done = [m[v] * scale[v] for v in top]
        out += [jnp.where(lane < 8 * v + 8, u, 0.0) for v, u in zip(top, done)]
        if b + window + ahead < n:
            u = jnp.concatenate(done, 0)
            step = lax.dot_general(u, u, (((0,), (0,)), ((), ())), precision=EXACT, preferred_element_type=F32)
            for v in range(b + window + ahead, n):
                m[v] = m[v] - step[8 * v : 8 * v + 8]
    return out


def basis_kernel(gram, got, half, basis):
    place = lax.axis_index("op") // 2
    m = [gram[8 * v : 8 * v + 8, :] + got[8 * v : 8 * v + 8, :] for v in range(16)]
    inverse = jnp.concatenate(inverse_rows(m, 2, 2), 0)
    rows = half[pl.ds(pl.multiple_of(place * 32, 32), 32), :]
    basis[...] = math.sqrt(512) * lax.dot_general(
        rows, inverse, (((1,), (1,)), ((), ())), precision=EXACT, preferred_element_type=F32
    )


def exchanged(n_op, n_sec):
    pairs = []
    for s in range(n_sec - 1):
        flip = 8 if s == n_sec // 2 - 1 else 0
        for o in range(0, n_op, 2):
            up = o if s == 0 else o + 1
            down = o + 1 if s == n_sec - 2 else o
            pairs.append(((up ^ flip) * n_sec + s, o * n_sec + s + 1))
            pairs.append((down * n_sec + s + 1, ((o + 1) ^ flip) * n_sec + s))
    for o in range(0, n_op, 2):
        pairs.append(((o + 1) * n_sec, o * n_sec))
        pairs.append((o * n_sec + n_sec - 1, (o + 1) * n_sec + n_sec - 1))
    return pairs


def body(psi, left_env, right_env, pair_code, sketch):
    terms = left_env.shape[0]
    n_op, n_sec = lax.axis_size("op"), lax.axis_size("sec")
    swap = [(i, i ^ 1) for i in range(n_op)]
    near = lax.ppermute(psi[0], ("op", "sec"), exchanged(n_op, n_sec))
    hbm = functools.partial(pltpu.with_memory_space_constraint, memory_space=pltpu.HBM)
    products = ((512, 512 * terms), BF)
    left, right, sketch, inner = call(
        load_kernel,
        "load",
        [SMEM] + [HBM] * 4,
        [((terms, 2, 8, 32, 512), BF), ((terms * 512, 512), BF), ((512, 128), BF), products],
        [pltpu.VMEM((512, 512), BF), pltpu.SemaphoreType.DMA((5,))],
        limit=4,
        bytes_accessed=18 * MIB,
    )(
        pair_code,
        hbm(left_env.reshape(terms, 8, 2, 32, 512)),
        hbm(right_env.reshape(terms * 512, 512)),
        hbm(psi[0]),
        hbm(sketch[0]),
    )
    near, left, right, sketch, inner = lax.optimization_barrier((near, left, right, sketch, inner))
    far = lax.ppermute(near, "op", swap)
    flops = 2 * 512**3 * terms
    (inner,) = call(
        near_kernel, "near", [SMEM] + [VMEM] * 3, [products], limit=4, flops=flops // 3, aliases={3: 0}
    )(pair_code, near, left, inner)
    inner, other = call(
        far_kernel,
        "far",
        [SMEM] + [VMEM] * 5,
        [products, ((256, 640), BF)],
        limit=6,
        flops=flops,
        aliases={5: 0},
    )(pair_code, far, left, right, sketch, inner)
    got = lax.ppermute(other, "op", swap)
    (mine,) = call(mine_kernel, "mine", [VMEM] * 3, [((256, 640), F32)], limit=6, flops=flops // 2)(
        inner, right, sketch
    )
    (packed,) = call(pack_kernel, "pack", [VMEM] * 2, [((8, 384, 128), BF)])(mine, got)
    groups = [[2 * p + c for p in CHIPS] for c in range(2)]
    parts = lax.all_to_all(packed, "op", 0, 0, axis_index_groups=groups, tiled=True)
    half, gram = call(sum_kernel, "gram", [VMEM], [((256, 128), F32), ((128, 128), F32)])(parts)
    other_gram = lax.ppermute(gram, "op", swap)
    (sigma,) = call(sigma_kernel, "sigma", [VMEM], [((32, 512), BF)], bytes_accessed=4 * MIB)(parts)
    (basis,) = call(basis_kernel, "basis", [VMEM] * 3, [((32, 128), F32)])(gram, other_gram, half)
    return sigma, basis


def solution(mesh):
    in_specs = (
        P("sec", None, None),
        P("op", "sec", None, None),
        P("op", "sec", None, None),
        P("op"),
        P("sec", None, None),
    )
    out_specs = (P("op", "sec"), P("op", "sec"))
    return jax.shard_map(body, mesh=mesh, in_specs=in_specs, out_specs=out_specs, check_vma=False)
```

```python
import functools
import math

import jax
import jax.numpy as jnp
from jax import lax
from jax.experimental import pallas as pl
from jax.experimental.pallas import tpu as pltpu
from jax.sharding import PartitionSpec as P

BF = jnp.bfloat16
F32 = jnp.float32
EXACT = lax.Precision.HIGHEST
HBM = pl.BlockSpec(memory_space=pltpu.HBM)
VMEM = pl.BlockSpec(memory_space=pltpu.VMEM)
SMEM = pl.BlockSpec(memory_space=pltpu.SMEM)
MIB = 2**20
CHIPS = (0, 4, 5, 1, 2, 6, 7, 3)


def call(kernel, name, in_specs, outs, scratch=(), limit=8, flops=1000, bytes_accessed=1000, aliases={}):
    return pl.pallas_call(
        kernel,
        in_specs=in_specs,
        out_specs=[VMEM] * len(outs),
        out_shape=[jax.ShapeDtypeStruct(shape, dtype) for shape, dtype in outs],
        scratch_shapes=scratch,
        input_output_aliases=aliases,
        compiler_params=pltpu.CompilerParams(vmem_limit_bytes=limit * MIB),
        cost_estimate=pl.CostEstimate(flops=flops, bytes_accessed=bytes_accessed, transcendentals=0),
        name=name,
    )


def times(inner, left, t, source):
    rows = left[t].reshape(512, 512)
    inner[:, 512 * t : 512 * t + 512] = jnp.dot(rows, source[...], preferred_element_type=F32).astype(BF)


def load_kernel(code, left, right, psi, sketch, lout, rout, sout, inner, here, sems):
    core = lax.axis_index("op") % 2
    sec, last = lax.axis_index("sec"), lax.axis_size("sec") - 1
    copies = [
        pltpu.make_async_copy(psi, here, sems.at[0]),
        pltpu.make_async_copy(left.at[:, :, core], lout.at[:, 0], sems.at[1]),
        pltpu.make_async_copy(left.at[:, :, 1 - core], lout.at[:, 1], sems.at[2]),
        pltpu.make_async_copy(right, rout, sems.at[3]),
        pltpu.make_async_copy(sketch, sout, sems.at[4]),
    ]
    for copy in copies:
        copy.start()
    for copy in copies[:3]:
        copy.wait()
    for t in range(left.shape[0]):
        k = code[t]

        @pl.when(k == 1)
        def _():
            times(inner, lout, t, here)

        @pl.when(((k == 2) & (sec == 0)) | ((k == 0) & (sec == last)))
        def _():
            inner[:, 512 * t : 512 * t + 512] = jnp.zeros((512, 512), BF)

    for copy in copies[3:]:
        copy.wait()


def multiply(code, inner, left, source, wanted):
    sec, last = lax.axis_index("sec"), lax.axis_size("sec") - 1
    for t in range(left.shape[0]):
        k = code[t]
        empty = ((k == 2) & (sec == 0)) | ((k == 0) & (sec == last))

        @pl.when((k == wanted) & jnp.logical_not(empty))
        def _():
            times(inner, left, t, source)


def near_kernel(code, near, left, before, inner):
    core = lax.axis_index("op") % 2
    multiply(code, inner, left, near, jnp.where(core == 0, 2, 0))


def finish(inner, right, sketch, h, ref):
    total = jnp.dot(inner[256 * h : 256 * h + 256, :], right[...], preferred_element_type=F32)
    total = total * (1.0 / math.sqrt(128))
    ref[:, :512] = total.astype(ref.dtype)
    ref[:, 512:] = jnp.dot(total.astype(BF), sketch[...], preferred_element_type=F32).astype(ref.dtype)


def far_kernel(code, far, left, right, sketch, before, inner, other):
    core = lax.axis_index("op") % 2
    multiply(code, inner, left, far, jnp.where(core == 0, 0, 2))
    finish(inner, right, sketch, 1, other)


def mine_kernel(inner, right, sketch, mine):
    finish(inner, right, sketch, 0, mine)


def pack_kernel(mine, got, out):
    for i, p in enumerate(CHIPS):
        rows = pl.ds(32 * p, 32)
        for j in range(4):
            cols = pl.ds(128 * j, 128)
            out[i, 32 * j : 32 * j + 32, :] = (mine[rows, cols] + got[rows, cols].astype(F32)).astype(BF)
    some = (mine[:, 512:] + got[:, 512:].astype(F32)).astype(BF)
    for i in range(8):
        out[i, 128:, :] = some


def sum_kernel(got, half, gram):
    total = got[0, 128:, :].astype(F32)
    for p in range(1, 8):
        total += got[p, 128:, :].astype(F32)
    gram[...] = lax.dot_general(
        total, total, (((0,), (0,)), ((), ())), precision=EXACT, preferred_element_type=F32
    )
    half[...] = total


def sigma_kernel(got, sigma):
    for j in range(4):
        rows = pl.ds(32 * j, 32)
        total = got[0, rows, :].astype(F32)
        for p in range(1, 8):
            total += got[p, rows, :].astype(F32)
        sigma[:, 128 * j : 128 * j + 128] = total.astype(BF)


def inverse_rows(m, window, ahead):
    n, size = len(m), 8 * window
    row = lax.broadcasted_iota(jnp.int32, (8, 128), 0)
    lane = lax.broadcasted_iota(jnp.int32, (8, 128), 1)
    out = []
    for b in range(0, n, window):
        top, near, base = range(b, b + window), range(b, min(b + window + ahead, n)), 8 * b
        c = {v: [jnp.broadcast_to(m[v][:, base + k : base + k + 1], (8, 128)) for k in range(size)] for v in near}
        here = (lane >= base) & (lane < base + size)
        for v in range(b, n):
            m[v] = jnp.where(here, jnp.where(lane == row + 8 * v, 1.0, 0.0) if v in top else 0.0, m[v])
        scale = {v: jnp.zeros((8, 128), F32) for v in top}
        for k in range(size):
            h, i = b + k // 8, k % 8
            s = lax.rsqrt(jnp.broadcast_to(c[h][k][i : i + 1, :], (8, 128)))
            scale[h] = jnp.where(row == i, s, scale[h])
            below = [v for v in near if v >= h]
            f = {v: c[v][k] * (s * s) for v in below}
            f[h] = jnp.where(row > i, f[h], 0.0)
            for j in range(k + 1, size):
                q = jnp.broadcast_to(c[h][j][i : i + 1, :], (8, 128))
                for v in below:
                    c[v][j] = c[v][j] - f[v] * q
            pivot = jnp.broadcast_to(m[h][i : i + 1, :], (8, 128))
            for v in below:
                m[v] = m[v] - f[v] * pivot
        done = [m[v] * scale[v] for v in top]
        out += [jnp.where(lane < 8 * v + 8, u, 0.0) for v, u in zip(top, done)]
        if b + window + ahead < n:
            u = jnp.concatenate(done, 0)
            step = lax.dot_general(u, u, (((0,), (0,)), ((), ())), precision=EXACT, preferred_element_type=F32)
            for v in range(b + window + ahead, n):
                m[v] = m[v] - step[8 * v : 8 * v + 8]
    return out


def basis_kernel(gram, got, half, basis):
    place = lax.axis_index("op") // 2
    m = [gram[8 * v : 8 * v + 8, :] + got[8 * v : 8 * v + 8, :] for v in range(16)]
    inverse = jnp.concatenate(inverse_rows(m, 2, 3), 0)
    rows = half[pl.ds(pl.multiple_of(place * 32, 32), 32), :]
    basis[...] = math.sqrt(512) * lax.dot_general(
        rows, inverse, (((1,), (1,)), ((), ())), precision=EXACT, preferred_element_type=F32
    )


def exchanged(n_op, n_sec):
    pairs = []
    for s in range(n_sec - 1):
        flip = 8 if s == n_sec // 2 - 1 else 0
        for o in range(0, n_op, 2):
            up = o if s == 0 else o + 1
            down = o + 1 if s == n_sec - 2 else o
            pairs.append(((up ^ flip) * n_sec + s, o * n_sec + s + 1))
            pairs.append((down * n_sec + s + 1, ((o + 1) ^ flip) * n_sec + s))
    for o in range(0, n_op, 2):
        pairs.append(((o + 1) * n_sec, o * n_sec))
        pairs.append((o * n_sec + n_sec - 1, (o + 1) * n_sec + n_sec - 1))
    return pairs


def body(psi, left_env, right_env, pair_code, sketch):
    terms = left_env.shape[0]
    n_op, n_sec = lax.axis_size("op"), lax.axis_size("sec")
    swap = [(i, i ^ 1) for i in range(n_op)]
    near = lax.ppermute(psi[0], ("op", "sec"), exchanged(n_op, n_sec))
    hbm = functools.partial(pltpu.with_memory_space_constraint, memory_space=pltpu.HBM)
    products = ((512, 512 * terms), BF)
    left, right, sketch, inner = call(
        load_kernel,
        "load",
        [SMEM] + [HBM] * 4,
        [((terms, 2, 8, 32, 512), BF), ((terms * 512, 512), BF), ((512, 128), BF), products],
        [pltpu.VMEM((512, 512), BF), pltpu.SemaphoreType.DMA((5,))],
        limit=4,
        bytes_accessed=18 * MIB,
    )(
        pair_code,
        hbm(left_env.reshape(terms, 8, 2, 32, 512)),
        hbm(right_env.reshape(terms * 512, 512)),
        hbm(psi[0]),
        hbm(sketch[0]),
    )
    near, left, right, sketch, inner = lax.optimization_barrier((near, left, right, sketch, inner))
    far = lax.ppermute(near, "op", swap)
    flops = 2 * 512**3 * terms
    (inner,) = call(
        near_kernel, "near", [SMEM] + [VMEM] * 3, [products], limit=4, flops=flops // 3, aliases={3: 0}
    )(pair_code, near, left, inner)
    inner, other = call(
        far_kernel,
        "far",
        [SMEM] + [VMEM] * 5,
        [products, ((256, 640), BF)],
        limit=6,
        flops=flops,
        aliases={5: 0},
    )(pair_code, far, left, right, sketch, inner)
    got = lax.ppermute(other, "op", swap)
    (mine,) = call(mine_kernel, "mine", [VMEM] * 3, [((256, 640), F32)], limit=6, flops=flops // 2)(
        inner, right, sketch
    )
    (packed,) = call(pack_kernel, "pack", [VMEM] * 2, [((8, 384, 128), BF)])(mine, got)
    groups = [[2 * p + c for p in CHIPS] for c in range(2)]
    parts = lax.all_to_all(packed, "op", 0, 0, axis_index_groups=groups, tiled=True)
    half, gram = call(sum_kernel, "gram", [VMEM], [((256, 128), F32), ((128, 128), F32)])(parts)
    other_gram = lax.ppermute(gram, "op", swap)
    (sigma,) = call(sigma_kernel, "sigma", [VMEM], [((32, 512), BF)], bytes_accessed=4 * MIB)(parts)
    (basis,) = call(basis_kernel, "basis", [VMEM] * 3, [((32, 128), F32)])(gram, other_gram, half)
    return sigma, basis


def solution(mesh):
    in_specs = (
        P("sec", None, None),
        P("op", "sec", None, None),
        P("op", "sec", None, None),
        P("op"),
        P("sec", None, None),
    )
    out_specs = (P("op", "sec"), P("op", "sec"))
    return jax.shard_map(body, mesh=mesh, in_specs=in_specs, out_specs=out_specs, check_vma=False)
```
